32 devices in a mesh: dp: 8 (over z, y), vocab: 4 (over x, core).
Axes of the slice: x: 2, y: 2, z: 4, core: 2. Of those that a mesh axis runs over, the one named last changes fastest.
Arguments:
- gains_master: float32 [3, 2, 768], P(None, None, 'dp')
- gains_first: float32 [3, 2, 768], P(None, None, 'dp'), may hold values from -0.00015258789 to 0.00015258789
- gains_second: float32 [3, 2, 768], P(None, None, 'dp'), may hold values from 3e-09 to 3e-07
- entry_master: float32 [1, 768, 5376], P(None, 'dp'), may hold values from -0.21875 to 0.21875
- entry_first: float32 [1, 768, 5376], P(None, 'dp'), may hold values from -0.00015258789 to 0.00015258789
- entry_second: float32 [1, 768, 5376], P(None, 'dp'), may hold values from 3e-11 to 1e-09
- merge_master: float32 [1, 3840, 768], P(None, 'dp')
- merge_first: float32 [1, 3840, 768], P(None, 'dp'), may hold values from -0.00015258789 to 0.00015258789
- merge_second: float32 [1, 3840, 768], P(None, 'dp'), may hold values from 3e-11 to 1e-09
- embed_master: float32 [50304, 768], P('vocab', 'dp'), may hold values from -4 to 4
- embed_first: float32 [50304, 768], P('vocab', 'dp'), may hold values from -0.00015258789 to 0.00015258789
- embed_second: float32 [50304, 768], P('vocab', 'dp'), may hold values from 3e-11 to 1e-09
- head_master: float32 [768, 50304], P('dp', 'vocab'), may hold values from -0.21875 to 0.21875
- head_first: float32 [768, 50304], P('dp', 'vocab'), may hold values from -0.00015258789 to 0.00015258789
- head_second: float32 [768, 50304], P('dp', 'vocab'), may hold values from 3e-11 to 1e-09
- tokens: int32 [32, 256], P(('dp', 'vocab')), may hold values from 0 to 50303
- seq_lengths: int32 [32], P(('dp', 'vocab')), may hold values from 33 to 256, as said below
- answer_len: int32 [32], P(('dp', 'vocab')), may hold values from 8 to 32, as said below
- ref_logp: float32 [32, 32], P(('dp', 'vocab')), may hold values from -12.9 to -9.9
- pairing: int32 [32], replicated, may hold values from 0 to 31, each once
- deal: int32 [32], replicated, may hold values from 0 to 31, each once
Outputs:
- loss: float32 [], replicated
- grad_norm: float32 [], replicated
- gains_step: float32 [3, 2, 768], P(None, None, 'dp')
- gains_first_new: float32 [3, 2, 768], P(None, None, 'dp')
- gains_second_new: float32 [3, 2, 768], P(None, None, 'dp')
- entry_new: float32 [1, 768, 5376], P(None, 'dp')
- entry_first_new: float32 [1, 768, 5376], P(None, 'dp')
- entry_second_new: float32 [1, 768, 5376], P(None, 'dp')
- entry_copy: bfloat16 [1, 768, 5376], P(None, 'dp')
- merge_new: float32 [1, 3840, 768], P(None, 'dp')
- merge_first_new: float32 [1, 3840, 768], P(None, 'dp')
- merge_second_new: float32 [1, 3840, 768], P(None, 'dp')
- merge_copy: bfloat16 [1, 3840, 768], P(None, 'dp')
- embed_new: float32 [50304, 768], P('vocab', 'dp')
- embed_first_new: float32 [50304, 768], P('vocab', 'dp')
- embed_second_new: float32 [50304, 768], P('vocab', 'dp')
- embed_copy: bfloat16 [50304, 768], P('vocab', 'dp')
- head_new: float32 [768, 50304], P('dp', 'vocab')
- head_first_new: float32 [768, 50304], P('dp', 'vocab')
- head_second_new: float32 [768, 50304], P('dp', 'vocab')
- head_copy: bfloat16 [768, 50304], P('dp', 'vocab')
The draws below stay inside these ranges and needn't reach their ends.
Inputs may be any that keep to these rules, and one draw needn't show every extreme that they name: Loaded row r holds a sequence of seq_lengths[r] tokens; its last 32 slots are its completion. Only the first answer_len[r] completion slots of loaded row r count. pairing[2q] is the chosen and pairing[2q + 1] the rejected batch sequence of pair q; every batch sequence is in exactly one pair. Batch sequence b is loaded row deal[b]; each loaded row is one batch sequence.
All inputs are finite; a program needn't handle non-finite values.
Results may differ from the reference program's by a relative error of at most 0.012.
The reference program's roundings to bfloat16 on the way count: a program that leaves them out, or rounds other values in their place, can miss the bound.
Values may be sent and summed in bfloat16 or wider, within the bound.
No kernel may reach another device: no remote copies, remote signals or barrier semaphores. Data moves between devices by JAX's collectives and lax.ppermute only.
A program may use at most 384 MiB of HBM per device.

```python
import math
from functools import partial
import jax
import jax.numpy as jnp
import numpy as np
from jax import lax

D = 768
H = 12
HD = 64
ROT = 16
FF = 3072
V = 50304
L = 1
SEQ_LEN = 256
COMP = 32
NSEQ = 32
NPAIR = 16


def draw_gains_master(key, part):
    gain_key, shift_key = jax.random.split(key)
    gains = jax.random.uniform(gain_key, (2 * L + 1, 1, D), jnp.float32, 0.6, 1.4)
    shifts = 0.3 * jax.random.normal(shift_key, (2 * L + 1, 1, D), jnp.float32)
    return jnp.concatenate([gains, shifts], 1)


def draw_merge_master(key, part):
    attn_key, mlp_key = jax.random.split(key)
    attn_rows = jax.random.normal(attn_key, (L, D, D), jnp.float32) * (4.0 / math.sqrt(D))
    mlp_rows = jax.random.normal(mlp_key, (L, FF, D), jnp.float32) / math.sqrt(FF)
    return jnp.concatenate([attn_rows, mlp_rows], 1)


def forced_ints(key, lowest, highest):
    base_key, first_key, second_key = jax.random.split(key, 3)
    values = jax.random.randint(base_key, (NSEQ,), lowest, highest + 1)
    first_pick = jax.random.randint(first_key, (), 0, NSEQ)
    second_pick = (first_pick + 1 + jax.random.randint(second_key, (), 0, NSEQ - 1)) % NSEQ
    values = values.at[first_pick].set(lowest).at[second_pick].set(highest)
    return values.astype(jnp.int32)


def draw_seq_lengths(key, part):
    return forced_ints(jax.random.fold_in(key, 11), COMP + 1, SEQ_LEN)


def draw_answer_len(key, part):
    return forced_ints(jax.random.fold_in(key, 23), max(1, COMP // 4), COMP)


def touch_ends(entries, own_key, smallest, largest):
    extent = entries.shape
    index_at = [jax.random.randint(jax.random.fold_in(own_key, axis), (), 0, extent[axis]) for axis in range(len(extent))]
    entries = entries.at[tuple(index_at)].set(smallest)
    longest = extent.index(max(extent))
    index_at[longest] = (index_at[longest] + 1) % extent[longest]
    return entries.at[tuple(index_at)].set(largest)


def block_levels(rng, extent, shards, smallest, largest):
    loudness = 1.0
    for dim, parts in shards:
        heights = jax.random.uniform(jax.random.fold_in(jax.random.fold_in(rng, 6), dim), (parts,), jnp.float32, smallest / len(shards), largest / len(shards))
        loudness = loudness * jnp.repeat(jnp.exp(heights), extent[dim] // parts).reshape((-1,) + (1,) * (len(extent) - 1 - dim))
    return loudness


def rank_bounds(count, lean):
    loads = [(1 << 20) // math.isqrt(grade ** lean) + 1 for grade in range(1, count + 1)]
    scale = 1 + sum(loads) // (1 << 30)
    return np.cumsum(np.array([max(1, weight // scale) for weight in loads]))


def skewed_ids(own_key, dims, number_of, lean):
    table = rank_bounds(number_of, lean)
    pick = jax.random.randint(jax.random.fold_in(own_key, 1), dims, 0, int(table[number_of - 1]))
    grade = jnp.searchsorted(jnp.asarray(table, jnp.int32), pick, side="right")
    return jax.random.permutation(jax.random.fold_in(own_key, 2), number_of)[grade].astype(jnp.int32)


def noise(rng, dims, width, limit, cuts=(), kind=jnp.bfloat16):
    result = jax.random.normal(rng, dims, jnp.float32) * width
    if len(cuts) > 0:
        result = block_levels(rng, dims, cuts, -0.22, 0.18) * result
    return jnp.clip(result, min=-limit, max=limit).astype(kind)


def setup_inputs(seed: int = 0) -> dict:
    keys = jax.random.split(jax.random.key(seed), 22)
    gains_master = draw_gains_master(jax.random.fold_in(keys[21], 71), 0)
    gains_first = noise(keys[1], (2 * L + 1, 2, D), (1e-5), 0.00015258789, ((2, 8),), jnp.float32)
    gains_second = jnp.clip(jnp.exp(math.log(3.000000106112566e-07) - 4.6051702 * jax.random.uniform(keys[2], (2 * L + 1, 2, D), jnp.float32) ** block_levels(keys[2], (2 * L + 1, 2, D), ((2, 8),), -0.2, 0.2)), 3.000000026176508e-09, 3.000000106112566e-07)
    entry_master = noise(keys[3], (L, D, 3 * D + FF), D ** -0.5, 0.21875, ((1, 8),), jnp.float32)
    entry_first = noise(keys[4], (L, D, 3 * D + FF), (1e-5), 0.00015258789, ((1, 8),), jnp.float32)
    entry_second = jnp.clip(jnp.exp(math.log(9.999999717180685e-10) - 3.506558 * jax.random.uniform(keys[5], (L, D, 3 * D + FF), jnp.float32) ** block_levels(keys[5], (L, D, 3 * D + FF), ((1, 8),), -0.2, 0.2)), 2.999999901276418e-11, 9.999999717180685e-10)
    merge_master = draw_merge_master(jax.random.fold_in(keys[21], 71), 0)
    merge_first = noise(keys[7], (L, D + FF, D), (1e-5), 0.00015258789, ((1, 8),), jnp.float32)
    merge_second = jnp.clip(jnp.exp(math.log(9.999999717180685e-10) - 3.506558 * jax.random.uniform(keys[8], (L, D + FF, D), jnp.float32) ** block_levels(keys[8], (L, D + FF, D), ((1, 8),), -0.2, 0.2)), 2.999999901276418e-11, 9.999999717180685e-10)
    embed_master = noise(keys[9], (V, D), 0.3, 4.0, ((0, 4), (1, 8)), jnp.float32)
    embed_first = noise(keys[10], (V, D), (1e-5), 0.00015258789, ((0, 4), (1, 8)), jnp.float32)
    embed_second = jnp.clip(jnp.exp(math.log(9.999999717180685e-10) - 3.506558 * jax.random.uniform(keys[11], (V, D), jnp.float32) ** block_levels(keys[11], (V, D), ((0, 4), (1, 8)), -0.2, 0.2)), 2.999999901276418e-11, 9.999999717180685e-10)
    head_master = noise(keys[12], (D, V), D ** -0.5, 0.21875, ((0, 8), (1, 4)), jnp.float32)
    head_first = noise(keys[13], (D, V), (1e-5), 0.00015258789, ((0, 8), (1, 4)), jnp.float32)
    head_second = jnp.clip(jnp.exp(math.log(9.999999717180685e-10) - 3.506558 * jax.random.uniform(keys[14], (D, V), jnp.float32) ** block_levels(keys[14], (D, V), ((0, 8), (1, 4)), -0.2, 0.2)), 2.999999901276418e-11, 9.999999717180685e-10)
    tokens = touch_ends(skewed_ids(keys[15], (NSEQ, SEQ_LEN), V, 2), jax.random.fold_in(keys[15], 3), 0, V - 1).astype(jnp.int32)
    seq_lengths = draw_seq_lengths(jax.random.fold_in(keys[21], 71), 0)
    answer_len = draw_answer_len(jax.random.fold_in(keys[21], 71), 0)
    ref_logp = jnp.clip(-12.9 + 3.0 * jax.random.uniform(keys[18], (NSEQ, COMP), jnp.float32) ** block_levels(keys[18], (NSEQ, COMP), ((0, 32),), -0.2, 0.2), -12.9, -9.9)
    pairing = jax.random.permutation(keys[19], NSEQ).astype(jnp.int32)
    deal = jax.random.permutation(keys[20], NSEQ).astype(jnp.int32)
    return {"gains_master": gains_master, "gains_first": gains_first, "gains_second": gains_second, "entry_master": entry_master, "entry_first": entry_first, "entry_second": entry_second, "merge_master": merge_master, "merge_first": merge_first, "merge_second": merge_second, "embed_master": embed_master, "embed_first": embed_first, "embed_second": embed_second, "head_master": head_master, "head_first": head_first, "head_second": head_second, "tokens": tokens, "seq_lengths": seq_lengths, "answer_len": answer_len, "ref_logp": ref_logp, "pairing": pairing, "deal": deal}


@jax.custom_vjp
def low(v):
    return lax.optimization_barrier(v.astype(jnp.bfloat16)).astype(jnp.float32)

@jax.custom_vjp
def low_back(v):
    return v

def low_keep(v):
    return (low(v), None)

def low_pass(kept, grad):
    return (grad,)

def back_keep(v):
    return (v, None)

def back_low(kept, grad):
    return (low(grad),)
low.defvjp(low_keep, low_pass)
low_back.defvjp(back_keep, back_low)
DPO_BETA = 0.1
CLIP_SHARE = 0.33
LEARN_RATE = 0.03
WEIGHT_DECAY = 0.1
FIRST_DECAY = 0.9
SECOND_DECAY = 0.95
STEP_NUMBER = 10.0
ADAM_EPSILON = 1e-08
NORM_EPSILON = 1e-05
HIGHEST = lax.Precision.HIGHEST

def layer_norm(values, gain, shift):
    centre = lax.optimization_barrier(jnp.mean(values, -1, keepdims=True))
    centred = values - centre
    spread = lax.optimization_barrier(jnp.mean(centred * centred, -1, keepdims=True))
    return centred * lax.rsqrt(spread + NORM_EPSILON) * gain + shift

def rope_tables():
    positions = jnp.arange(SEQ_LEN).astype(jnp.float32)
    frequency = 10000.0 ** (-jnp.arange(ROT // 2).astype(jnp.float32) * 2.0 / ROT)
    angles = positions[:, None] * frequency[None, :]
    return (jnp.cos(angles), jnp.sin(angles))

def rotate(heads, cosine, sine):
    half_rot = ROT // 2
    front_part = heads[..., :half_rot]
    back_part = heads[..., half_rot:ROT]
    rest_part = heads[..., ROT:]
    cosine_col = cosine[:, None, :]
    sine_col = sine[:, None, :]
    return jnp.concatenate([front_part * cosine_col - back_part * sine_col, back_part * cosine_col + front_part * sine_col, rest_part], -1)

def attend_block(query_block, key_rows, value_rows, offset):
    scaling = HD ** (-0.5)
    scores = low_back(jnp.einsum('qhd,khd->hqk', query_block, key_rows, precision=HIGHEST) * scaling)
    query_pos = offset + jnp.arange(query_block.shape[0])
    key_pos = jnp.arange(key_rows.shape[0])
    allowed = key_pos[None, :] <= query_pos[:, None]
    scores = jnp.where(allowed[None], scores, -1e+30)
    weights = low(jax.nn.softmax(scores, axis=-1))
    return jnp.einsum('hqk,khd->qhd', weights, value_rows, precision=HIGHEST)

def attend(queries, key_rows, value_rows):
    block_rows = min(512, SEQ_LEN)
    pieces = []
    for block_index in range(SEQ_LEN // block_rows):
        begin = block_index * block_rows
        finish = begin + block_rows
        block_fn = jax.checkpoint(partial(attend_block, offset=begin))
        pieces.append(block_fn(queries[begin:finish], key_rows[:finish], value_rows[:finish]))
    return jnp.concatenate(pieces, 0)

def sequence_score(copies, token_row, start_pos, live_count, ref_row):
    norm_copy, entry_copy, merge_copy, embed_copy, head_copy = copies
    cosine, sine = rope_tables()
    head_shape = (SEQ_LEN, H, HD)
    hidden_state = low_back(jnp.take(embed_copy, token_row, axis=0))
    for layer_index in range(L):
        norm_pair = norm_copy[2 * layer_index:2 * layer_index + 2]
        attn_in = low(layer_norm(hidden_state, norm_pair[0, 0], norm_pair[0, 1]))
        mlp_in = low(layer_norm(hidden_state, norm_pair[1, 0], norm_pair[1, 1]))
        joined_qkv = low_back(jnp.dot(attn_in, entry_copy[layer_index][:, :3 * D], precision=HIGHEST))
        up_proj = low_back(jnp.dot(mlp_in, entry_copy[layer_index][:, 3 * D:], precision=HIGHEST))
        queries = low(rotate(joined_qkv[:, :D].reshape(head_shape), cosine, sine))
        key_rows = low(rotate(joined_qkv[:, D:2 * D].reshape(head_shape), cosine, sine))
        value_rows = low(joined_qkv[:, 2 * D:].reshape(head_shape))
        attn_mixed = low(low_back(attend(queries, key_rows, value_rows).reshape(SEQ_LEN, D)))
        activated = low(jax.nn.gelu(up_proj, approximate=False))
        branch = low_back(jnp.dot(jnp.concatenate([attn_mixed, activated], 1), merge_copy[layer_index], precision=HIGHEST))
        hidden_state = hidden_state + branch
    final_norm = layer_norm(hidden_state, norm_copy[2 * L, 0], norm_copy[2 * L, 1])
    comp_rows = low(lax.dynamic_slice_in_dim(final_norm, start_pos - 1, COMP, 0))
    logits = low_back(jnp.dot(comp_rows, head_copy, precision=HIGHEST))
    targets = lax.dynamic_slice_in_dim(token_row, start_pos, COMP, 0)
    picked = jnp.take_along_axis(logits, targets[:, None], axis=1)[:, 0]
    logprob = picked - jax.scipy.special.logsumexp(logits, axis=1)
    live_mask = (jnp.arange(COMP) < live_count).astype(logprob.dtype)
    return jnp.sum(live_mask * (logprob - ref_row))

def total_loss(copies, tokens, seq_lengths, answer_len, ref_logp, pairing, deal):
    batch_tokens = jnp.take(tokens, deal, axis=0)
    batch_start = (jnp.take(seq_lengths, deal, axis=0) - COMP).astype(jnp.int32)
    batch_live = jnp.take(answer_len, deal, axis=0)

    def one_sequence(inputs):
        return sequence_score(copies, inputs[0], inputs[1], inputs[2], inputs[3])
    scores = lax.map(jax.checkpoint(one_sequence), (batch_tokens, batch_start, batch_live, ref_logp))
    margin = DPO_BETA * (scores[pairing[0::2]] - scores[pairing[1::2]])
    return jnp.mean(-jax.nn.log_sigmoid(margin))

def adam_update(master, first_moment, second_moment, gradient, factor, decay_rate):
    scaled = gradient * factor
    new_first = FIRST_DECAY * first_moment + (1.0 - FIRST_DECAY) * scaled
    new_second = SECOND_DECAY * second_moment + (1.0 - SECOND_DECAY) * scaled * scaled
    first_hat = new_first / (1.0 - FIRST_DECAY ** STEP_NUMBER)
    second_hat = new_second / (1.0 - SECOND_DECAY ** STEP_NUMBER)
    change = -LEARN_RATE * (first_hat / (jnp.sqrt(second_hat) + ADAM_EPSILON) + decay_rate * master)
    new_master = master + change
    return (new_master, new_first, new_second, change)

def reference(gains_master, gains_first, gains_second, entry_master, entry_first, entry_second, merge_master, merge_first, merge_second, embed_master, embed_first, embed_second, head_master, head_first, head_second, tokens, seq_lengths, answer_len, ref_logp, pairing, deal):
    masters = (gains_master, entry_master, merge_master, embed_master, head_master)
    copies = tuple((weight.astype(jnp.bfloat16).astype(jnp.float32) for weight in masters))

    def loss_of(weights):
        return total_loss(weights, tokens, seq_lengths, answer_len, ref_logp, pairing, deal)
    loss, pullback = jax.vjp(loss_of, copies)
    grads = pullback(jnp.ones_like(loss))[0]
    squares = jnp.sum(grads[0] * grads[0]) + jnp.sum(grads[1] * grads[1]) + jnp.sum(grads[2] * grads[2]) + jnp.sum(grads[3] * grads[3]) + jnp.sum(grads[4] * grads[4])
    grad_norm = jnp.sqrt(squares)
    clip_limit = CLIP_SHARE * DPO_BETA * math.sqrt(COMP * D / NPAIR)
    factor = jnp.minimum(1.0, clip_limit / (grad_norm + 1e-06))
    gains = adam_update(gains_master, gains_first, gains_second, grads[0], factor, 0.0)
    entry = adam_update(entry_master, entry_first, entry_second, grads[1], factor, WEIGHT_DECAY)
    merge = adam_update(merge_master, merge_first, merge_second, grads[2], factor, WEIGHT_DECAY)
    embed = adam_update(embed_master, embed_first, embed_second, grads[3], factor, WEIGHT_DECAY)
    head = adam_update(head_master, head_first, head_second, grads[4], factor, WEIGHT_DECAY)
    return (loss, grad_norm, gains[3], gains[1], gains[2], entry[0], entry[1], entry[2], entry[0].astype(jnp.bfloat16), merge[0], merge[1], merge[2], merge[0].astype(jnp.bfloat16), embed[0], embed[1], embed[2], embed[0].astype(jnp.bfloat16), head[0], head[1], head[2], head[0].astype(jnp.bfloat16))
```

```python
import math

import jax
import jax.numpy as jnp
import numpy as np
from jax import lax
from jax.experimental import pallas as pl
from jax.experimental.pallas import tpu as pltpu
from jax.sharding import PartitionSpec as P

D = 768
H = 12
HD = 64
ROT = 16
FF = 3072
COMP = 32
QKV = 3 * D

DPO_BETA = 0.1
CLIP_SHARE = 0.33
LEARN_RATE = 0.03
WEIGHT_DECAY = 0.1
FIRST_DECAY = 0.9
SECOND_DECAY = 0.95
STEP_NUMBER = 10.0
ADAM_EPSILON = 1e-08
NORM_EPSILON = 1e-05

F32 = jnp.float32
BF16 = jnp.bfloat16
ALL = ("dp", "vocab")
LANES = 128
ACCUMULATORS = 4


def round_up(value, unit):
    return -(-value // unit) * unit


def rounded(values):
    return lax.reduce_precision(values, 8, 7)


def dot(left, right, left_dim, right_dim):
    return lax.dot_general(
        left, right, (((left_dim,), (right_dim,)), ((), ())), preferred_element_type=F32
    )


def gather_kernel(ids_ref, table_ref, out_ref, store, rows):
    total, width = table_ref.shape
    block = out_ref.shape[0]

    @pl.when(pl.program_id(0) == 0)
    def _():
        store[pl.ds(0, total), pl.ds(0, width)] = table_ref[...]
        store[pl.ds(total, 8), :] = jnp.zeros((8, store.shape[1]), F32)

    base = pl.program_id(0) * block

    def step(i, carry):
        first = pl.multiple_of(i * 8, 8)
        for k in range(8):
            rows[pl.ds(first + k, 1), :] = store[pl.ds(ids_ref[base + first + k], 1), :]
        return carry

    lax.fori_loop(0, block // 8, step, 0, unroll=2)
    out_ref[...] = rows[:, :width].astype(out_ref.dtype)


def gather_rows(table, ids, block=1024):
    count = ids.shape[0]
    total, width = table.shape
    return pl.pallas_call(
        gather_kernel,
        out_shape=jax.ShapeDtypeStruct((count, width), BF16),
        grid_spec=pltpu.PrefetchScalarGridSpec(
            num_scalar_prefetch=1,
            grid=(count // block,),
            in_specs=[
                pl.BlockSpec((total, width), lambda i, s: (0, 0), pipeline_mode=pl.Buffered(1))
            ],
            out_specs=pl.BlockSpec((block, width), lambda i, s: (i, 0)),
            scratch_shapes=[
                pltpu.VMEM((total + 8, LANES), F32),
                pltpu.VMEM((block, LANES), F32),
            ],
        ),
        compiler_params=pltpu.CompilerParams(vmem_limit_bytes=50 << 20),
        name="gather_rows",
    )(ids, table)


def scatter_kernel(ids_ref, rows_ref, out_ref, rows, *sums):
    total, width = out_ref.shape
    block = rows_ref.shape[0]
    step_id = pl.program_id(0)

    @pl.when(step_id == 0)
    def _():
        for part in sums:
            part[...] = jnp.zeros_like(part)

    rows[:, pl.ds(0, width)] = rows_ref[...].astype(F32)
    base = step_id * block

    def step(i, carry):
        first = pl.multiple_of(i * 8, 8)
        for k in range(8):
            part = sums[k % len(sums)]
            at = ids_ref[base + first + k]
            part[pl.ds(at, 1), :] = part[pl.ds(at, 1), :] + rows[pl.ds(first + k, 1), :]
        return carry

    lax.fori_loop(0, block // 8, step, 0)

    @pl.when(step_id == pl.num_programs(0) - 1)
    def _():
        result = sums[0][pl.ds(0, total), pl.ds(0, width)]
        for part in sums[1:]:
            result = result + part[pl.ds(0, total), pl.ds(0, width)]
        out_ref[...] = result


def scatter_rows(rows, ids, total, block=1024):
    count, width = rows.shape
    return pl.pallas_call(
        scatter_kernel,
        out_shape=jax.ShapeDtypeStruct((total, width), F32),
        grid_spec=pltpu.PrefetchScalarGridSpec(
            num_scalar_prefetch=1,
            grid=(count // block,),
            in_specs=[pl.BlockSpec((block, width), lambda i, s: (i, 0))],
            out_specs=pl.BlockSpec(
                (total, width), lambda i, s: (0, 0), pipeline_mode=pl.Buffered(1)
            ),
            scratch_shapes=[pltpu.VMEM((block, LANES), F32)]
            + [pltpu.VMEM((total + 8, LANES), F32) for _ in range(ACCUMULATORS)],
        ),
        compiler_params=pltpu.CompilerParams(vmem_limit_bytes=55 << 20),
        name="scatter_rows",
    )(ids, rows)


def flip(value, bit):
    count = lax.axis_size("vocab")
    return lax.ppermute(value, "vocab", [(i, i ^ bit) for i in range(count)])


def dp_swap(blocks):
    return lax.all_to_all(blocks, "dp", 0, 0, tiled=True)


def dp_gather(value):
    count = lax.axis_size("dp")
    return dp_swap(jnp.broadcast_to(value[None], (count,) + value.shape))


def all_gather_small(value):
    count = lax.axis_size("dp") * lax.axis_size("vocab")
    copies = jnp.broadcast_to(value[None], (count,) + value.shape)
    return lax.all_to_all(copies, ALL, 0, 0, tiled=True)


def dp_swap_async(blocks, cuts):
    count = lax.axis_size("dp")
    if count > 8:
        whole = dp_swap(blocks)
        return [whole[..., a:b] for a, b in cuts]
    me = lax.axis_index("dp")

    def placed(buffers, block, index):
        return [
            lax.dynamic_update_index_in_dim(buffer, block[..., a:b], index, 0)
            for buffer, (a, b) in zip(buffers, cuts)
        ]

    buffers = [jnp.zeros(blocks.shape[:-1] + (b - a,), blocks.dtype) for a, b in cuts]
    received = []
    for shift in range(1, count):
        block = lax.dynamic_index_in_dim(blocks, (me + shift) % count, 0, keepdims=False)
        received.append(
            lax.ppermute(block, "dp", [(i, (i + shift) % count) for i in range(count)])
        )
    own = lax.dynamic_index_in_dim(blocks, me, 0, keepdims=False)
    buffers = placed(buffers, own, me)
    for shift in range(1, count):
        buffers = placed(buffers, received[shift - 1], (me - shift) % count)
    return buffers


def vocab_reduce(values):
    values = values[0].astype(F32) + flip(values[1].astype(BF16), 1).astype(F32)
    return values[0] + flip(values[1].astype(BF16), 2).astype(F32)


def vocab_gather(value):
    value = jnp.stack([value, flip(value, 2)])
    return jnp.stack([value, flip(value, 1)])


def normalize(values):
    centre = jnp.mean(values, -1, keepdims=True)
    centred = values - centre
    inverse = lax.rsqrt(jnp.mean(centred * centred, -1, keepdims=True) + NORM_EPSILON)
    return (centred * inverse, inverse)


def norm_back(grad_hat, normed, inverse):
    return inverse * (
        grad_hat
        - jnp.mean(grad_hat, -1, keepdims=True)
        - normed * jnp.mean(grad_hat * normed, -1, keepdims=True)
    )


def rope_tables(length):
    half = ROT // 2
    positions = np.arange(length).astype(np.float32)
    frequency = (10000.0 ** (-np.arange(half).astype(np.float32) * 2.0 / ROT)).astype(np.float32)
    angles = (positions[:, None] * frequency[None, :]).astype(np.float32)
    cosine, sine = np.cos(angles), np.sin(angles)
    keep = np.ones((length, HD), np.float32)
    keep[:, :half] = cosine
    keep[:, half:ROT] = cosine
    above = np.zeros((length, HD), np.float32)
    above[:, :half] = -sine
    below = np.zeros((length, HD), np.float32)
    below[:, half:ROT] = sine
    return jnp.asarray(np.stack([keep, above, below]))


def rotate(rows, tables, sign):
    half = ROT // 2
    count = rows.shape[1] // HD
    keep, above, below = [jnp.tile(table, (1, count)) for table in tables]
    up = jnp.concatenate([rows[:, half:], rows[:, :half]], 1)
    down = jnp.concatenate([rows[:, -half:], rows[:, :-half]], 1)
    return rows * keep + sign * (up * above + down * below)


def exact_gelu(values):
    return jax.nn.gelu(values, approximate=False)


def adam_update(master, first_moment, second_moment, gradient, factor, decay_rate):
    scaled = gradient * factor
    new_first = FIRST_DECAY * first_moment + (1.0 - FIRST_DECAY) * scaled
    new_second = SECOND_DECAY * second_moment + (1.0 - SECOND_DECAY) * scaled * scaled
    first_hat = new_first / (1.0 - FIRST_DECAY**STEP_NUMBER)
    second_hat = new_second / (1.0 - SECOND_DECAY**STEP_NUMBER)
    change = -LEARN_RATE * (first_hat / (jnp.sqrt(second_hat) + ADAM_EPSILON) + decay_rate * master)
    new_master = master + change
    return (new_master, new_first, new_second, change)


def body(
    gains_master,
    gains_first,
    gains_second,
    entry_master,
    entry_first,
    entry_second,
    merge_master,
    merge_first,
    merge_second,
    embed_master,
    embed_first,
    embed_second,
    head_master,
    head_first,
    head_second,
    tokens,
    seq_lengths,
    answer_len,
    ref_logp,
    pairing,
    deal,
):
    ndp = lax.axis_size("dp")
    nv = lax.axis_size("vocab")
    seqs = ndp * nv
    d_rank = lax.axis_index("dp")
    v_rank = lax.axis_index("vocab")
    core_bit = v_rank % 2
    length = tokens.shape[1]
    part = D // ndp
    quarter = embed_master.shape[0]
    merge_rows = merge_master.shape[1]
    merge_cols = round_up(merge_rows, 2 * LANES)
    head_cols = round_up(-(-head_master.shape[1] // ndp), LANES)
    entry = entry_master[0].astype(BF16)
    merge = merge_master[0].astype(BF16)

    qkv_weight = lax.all_gather(entry[:, :QKV], "dp", axis=0, tiled=True)
    head_blocks = jnp.pad(
        head_master.astype(BF16), ((0, 0), (0, head_cols * ndp - head_master.shape[1]))
    ).reshape(part, ndp, head_cols)
    up_blocks = jnp.pad(
        entry[:, 2 * D :].reshape(part, ndp, merge_rows),
        ((0, 0), (0, 0), (0, merge_cols - merge_rows)),
    )
    weight_blocks = jnp.concatenate([head_blocks, up_blocks], 2).transpose(1, 0, 2)
    head_weight, up_weight = dp_swap_async(
        weight_blocks, [(0, head_cols), (head_cols, head_cols + merge_rows)]
    )
    head_weight = head_weight.reshape(D, head_cols)
    up_weight = up_weight.reshape(D, merge_rows)

    pieces = [
        tokens.reshape(-1).astype(F32),
        rounded(gains_master).reshape(-1),
        ref_logp.reshape(-1),
        seq_lengths.astype(F32),
        answer_len.astype(F32),
    ]
    packed = jnp.concatenate(pieces)
    filled = packed.shape[0]
    packed = jnp.pad(packed, (0, round_up(filled, 8 * LANES) - filled)).reshape(-1, LANES)
    shared = all_gather_small(packed).reshape(seqs, -1)
    at = length
    load_tokens = shared[:, :at].astype(jnp.int32)
    gains_count = 6 * part
    gains_full = (
        shared.reshape(ndp, nv, -1)[:, 0, at : at + gains_count]
        .reshape(ndp, 3, 2, part)
        .transpose(1, 2, 0, 3)
        .reshape(3, 2, D)
    )
    at += gains_count
    ref_all = shared[:, at : at + COMP]
    at += COMP
    load_lengths = shared[:, at].astype(jnp.int32)
    load_live = shared[:, at + 1].astype(jnp.int32)

    offsets = jnp.array([0, 2, 1, 3])
    batch = jnp.arange(seqs)
    seq_rel = (jnp.arange(ndp)[None, :] * nv + (v_rank ^ offsets)[:, None]).reshape(-1)
    rel_of = offsets[v_rank ^ (batch % nv)] * ndp + batch // nv
    batch_start = jnp.take(load_lengths, deal, axis=0) - COMP
    batch_live = jnp.take(load_live, deal, axis=0)
    deal_rel = jnp.take(deal, seq_rel, axis=0)
    tokens_rel = jnp.take(load_tokens, deal_rel, axis=0)
    start_rel = jnp.take(load_lengths, deal_rel, axis=0) - COMP
    own = d_rank * nv + v_rank
    row0 = batch_start[own] - 1

    local = tokens_rel.reshape(-1) - v_rank * quarter
    ids = jnp.where((local >= 0) & (local < quarter), local, quarter)
    found = gather_rows(embed_master, ids).reshape(2, nv // 2, ndp, length, part)
    found = vocab_reduce(found).astype(BF16)
    state = dp_swap(found).transpose(1, 0, 2).reshape(length, D)
    state_sel = lax.dynamic_slice_in_dim(state, row0, COMP, 0)
    state = state.astype(F32)

    normed, inverse = normalize(state)
    attn_in = (normed * gains_full[0, 0] + gains_full[0, 1]).astype(BF16)
    attn_in_sel = lax.dynamic_slice_in_dim(attn_in, row0, COMP, 0)
    tables = rope_tables(length)
    tables_sel = lax.dynamic_slice_in_dim(tables, row0, COMP, 1)
    key_value = jnp.dot(attn_in, qkv_weight[:, D:], preferred_element_type=F32)
    query_flat = jnp.dot(attn_in_sel, qkv_weight[:, :D], preferred_element_type=F32)
    queries = rotate(query_flat, tables_sel, 1.0).astype(BF16).reshape(COMP, H, HD)
    keys = rotate(key_value[:, :D], tables, 1.0).astype(BF16).reshape(length, H, HD)
    values = key_value[:, D:].astype(BF16).reshape(length, H, HD)
    scaling = HD ** (-0.5)
    scores = jnp.einsum("qhd,khd->hqk", queries, keys, preferred_element_type=F32) * scaling
    allowed = jnp.arange(length)[None, :] <= row0 + jnp.arange(COMP)[:, None]
    scores = jnp.where(allowed[None], scores, -1e30)
    weights = jnp.exp(scores - jnp.max(scores, -1, keepdims=True))
    weights = weights / jnp.sum(weights, -1, keepdims=True)
    weights_low = weights.astype(BF16)
    mixed = jnp.einsum("hqk,khd->qhd", weights_low, values, preferred_element_type=F32)
    mixed = mixed.reshape(COMP, D).astype(BF16)

    mixed_blocks = jnp.pad(mixed, ((0, 0), (0, ndp * merge_rows - D))).reshape(
        COMP, ndp, merge_rows
    )
    sent = jnp.concatenate(
        [
            jnp.broadcast_to(state_sel[None], (ndp, COMP, D)),
            mixed_blocks.transpose(1, 0, 2),
        ],
        2,
    )
    got = dp_swap(sent).reshape(ndp * COMP, D + merge_rows)
    group_normed, _ = normalize(got[:, :D].astype(F32))
    mlp_in = (group_normed * gains_full[1, 0] + gains_full[1, 1]).astype(BF16)
    up_proj = jnp.dot(mlp_in, up_weight, preferred_element_type=F32)
    activated, gelu_pull = jax.vjp(exact_gelu, up_proj)
    is_mlp = (d_rank * merge_rows + jnp.arange(merge_rows) >= D)[None, :]
    joined = jnp.where(is_mlp, activated.astype(BF16), got[:, D:])
    branch = jnp.dot(joined, merge, preferred_element_type=F32)
    branch = dp_swap(branch.astype(BF16).reshape(ndp, COMP, D)).astype(F32).sum(0)

    final_hat, final_inverse = normalize(state_sel.astype(F32) + branch)
    final_gain = gains_full[2, 0]
    comp_rows = (final_hat * final_gain + gains_full[2, 1]).astype(BF16)
    rows = vocab_gather(dp_gather(comp_rows)).reshape(seqs * COMP, D)

    logits = jnp.dot(rows, head_weight, preferred_element_type=F32)
    slots = jnp.arange(length)[None, None, :] == (
        start_rel[:, None, None] + jnp.arange(COMP)[None, :, None]
    )
    targets = jnp.sum(jnp.where(slots, tokens_rel[:, None, :], 0), -1).reshape(-1)
    column = jnp.arange(head_cols)[None, :]
    valid = d_rank * head_cols + column < quarter
    is_target = (
        column + (v_rank * quarter + d_rank * head_cols) == targets[:, None]
    ) & valid
    top_local = jnp.max(jnp.where(valid, logits, -1e30), -1)
    total_local = jnp.sum(jnp.where(valid, jnp.exp(logits - top_local[:, None]), 0.0), -1)
    picked_local = jnp.sum(jnp.where(is_target, logits, 0.0), -1)
    stats = jnp.stack([top_local, total_local, picked_local]).reshape(3, seqs, COMP)
    stats = jnp.take(stats, rel_of, axis=1)
    stats = all_gather_small(stats.reshape(-1, LANES)).reshape(seqs, 3, seqs, COMP)
    top_all = jnp.max(stats[:, 0], 0)
    total_all = jnp.sum(stats[:, 1] * jnp.exp(stats[:, 0] - top_all[None]), 0)
    log_total = top_all + jnp.log(total_all)
    logprob = jnp.sum(stats[:, 2], 0) - log_total
    live = (jnp.arange(COMP)[None, :] < batch_live[:, None]).astype(F32)
    score = jnp.sum(live * (logprob - ref_all), 1)
    chosen = pairing[0::2]
    rejected = pairing[1::2]
    margin = DPO_BETA * (score[chosen] - score[rejected])
    loss = jnp.mean(-jax.nn.log_sigmoid(margin))
    pull = -DPO_BETA * jax.nn.sigmoid(-margin) / margin.shape[0]
    signs = (chosen[None, :] == batch[:, None]).astype(F32) - (
        rejected[None, :] == batch[:, None]
    ).astype(F32)
    coef = jnp.sum(pull[None, :] * signs, 1)
    row_coef = jnp.take(coef[:, None] * live, seq_rel, axis=0).reshape(-1, 1)
    row_total = jnp.take(log_total, seq_rel, axis=0).reshape(-1, 1)
    grad_logits = row_coef * (is_target.astype(F32) - jnp.exp(logits - row_total))
    grad_logits = jnp.where(valid, grad_logits, 0.0).astype(BF16)

    grad_head = dot(rows, grad_logits, 0, 0).astype(BF16).reshape(ndp, part, head_cols)
    (head_grad,) = dp_swap_async(grad_head, [(0, head_cols)])
    head_grad = (
        head_grad.transpose(1, 0, 2).reshape(part, ndp * head_cols)[:, :quarter].astype(F32)
    )
    grad_rows = dot(grad_logits, head_weight, 1, 1).reshape(2, nv // 2, ndp, COMP, D)
    grad_rows = vocab_reduce(grad_rows).astype(BF16)
    grad_final = dp_swap(grad_rows).astype(F32).sum(0)
    final_pair = jnp.stack([jnp.sum(grad_final * final_hat, 0), jnp.sum(grad_final, 0)])
    grad_next = norm_back(grad_final * final_gain, final_hat, final_inverse)

    grad_branch = dp_gather(grad_next.astype(BF16)).reshape(ndp * COMP, D)
    grad_merge = dot(joined, grad_branch, 0, 0)
    grad_joined = dot(grad_branch, merge, 1, 1)
    grad_up = jnp.where(is_mlp, gelu_pull(grad_joined)[0], 0.0).astype(BF16)
    grad_up_weight = dot(mlp_in, grad_up, 0, 0)
    grad_mlp = dot(grad_up, up_weight, 1, 1)
    sent = jnp.concatenate([grad_mlp.astype(BF16), grad_joined.astype(BF16)], 1)
    got = dp_swap(sent.reshape(ndp, COMP, D + merge_rows))
    grad_mlp_in = got[:, :, :D].astype(F32).sum(0)
    grad_mixed = got[:, :, D:].transpose(1, 0, 2).reshape(COMP, ndp * merge_rows)[:, :D]
    grad_mixed = grad_mixed.reshape(COMP, H, HD)

    grad_value = jnp.einsum("hqk,qhd->khd", weights_low, grad_mixed, preferred_element_type=F32)
    grad_weights = jnp.einsum("qhd,khd->hqk", grad_mixed, values, preferred_element_type=F32)
    grad_scores = (
        weights * (grad_weights - jnp.sum(weights * grad_weights, -1, keepdims=True))
    ).astype(BF16)
    grad_query = jnp.einsum("hqk,khd->qhd", grad_scores, keys, preferred_element_type=F32)
    grad_key = jnp.einsum("hqk,qhd->khd", grad_scores, queries, preferred_element_type=F32)
    grad_query = rotate((grad_query * scaling).reshape(COMP, D), tables_sel, -1.0).astype(BF16)
    grad_key = rotate((grad_key * scaling).reshape(length, D), tables, -1.0).astype(BF16)
    grad_kv = jnp.concatenate([grad_key, grad_value.reshape(length, D).astype(BF16)], 1)
    grad_q_weight = dot(attn_in_sel, grad_query, 0, 0)
    grad_kv_weight = dot(attn_in, grad_kv, 0, 0)
    grad_attn_in = dot(grad_kv, qkv_weight[:, D:], 1, 1)
    grad_attn_sel = dot(grad_query, qkv_weight[:, :D], 1, 1)
    sel_before = lax.dynamic_slice_in_dim(grad_attn_in, row0, COMP, 0)
    grad_attn_in = lax.dynamic_update_slice_in_dim(
        grad_attn_in, sel_before + grad_attn_sel, row0, 0
    )
    normed_sel = lax.dynamic_slice_in_dim(normed, row0, COMP, 0)
    grad_pairs = jnp.stack(
        [
            jnp.sum(grad_attn_in * normed, 0),
            jnp.sum(grad_attn_in, 0),
            jnp.sum(grad_mlp_in * normed_sel, 0),
            jnp.sum(grad_mlp_in, 0),
            final_pair[0],
            final_pair[1],
        ]
    )
    no_rows = jnp.zeros((length, D), F32)
    mlp_hat = lax.dynamic_update_slice_in_dim(
        no_rows, grad_mlp_in * gains_full[1, 0], row0, 0
    )
    next_rows = lax.dynamic_update_slice_in_dim(no_rows, grad_next, row0, 0)
    grad_hat = grad_attn_in * gains_full[0, 0] + mlp_hat
    grad_state = (next_rows + norm_back(grad_hat, normed, inverse)).astype(BF16)

    state_blocks = grad_state.reshape(length, ndp, part).transpose(1, 0, 2)
    state_rows = vocab_gather(dp_swap(state_blocks)).reshape(-1, part)
    embed_grad = scatter_rows(state_rows, ids, quarter)

    def half_of(value, index):
        size = value.shape[-1] // 2
        return lax.dynamic_slice_in_dim(value, index * size, size, value.ndim - 1)

    def core_reduce(value):
        other = half_of(value, 1 - core_bit).astype(BF16)
        return half_of(value, core_bit) + flip(other, 1).astype(F32)

    def cross_sum(value):
        low = rounded(value)
        return low + flip(value.astype(BF16), 2).astype(F32)

    def both_halves(value):
        other = flip(value, 1)
        first = jnp.where(core_bit == 0, value, other)
        second = jnp.where(core_bit == 0, other, value)
        return jnp.concatenate([first, second], -1)

    merge_half = cross_sum(core_reduce(grad_merge))
    up_half = cross_sum(
        core_reduce(jnp.pad(grad_up_weight, ((0, 0), (0, merge_cols - merge_rows))))
    )
    qkv_half = core_reduce(jnp.concatenate([grad_q_weight, grad_kv_weight], 1))
    sent = jnp.concatenate([qkv_half.astype(BF16), up_half.astype(BF16)], 1)
    got = dp_swap(sent.reshape(ndp, part, (QKV + merge_cols) // 2)).astype(F32)
    qkv_half = cross_sum(got[:, :, : QKV // 2].sum(0))
    up_half = got[:, :, QKV // 2 :]
    merge_grad = both_halves(merge_half)[None]
    up_grad = both_halves(up_half)[:, :, :merge_rows].transpose(1, 0, 2).reshape(part, -1)
    entry_grad = jnp.concatenate([both_halves(qkv_half), up_grad[:, D:]], 1)[None]
    gains_blocks = grad_pairs.reshape(6, ndp, part).transpose(1, 0, 2)
    gains_blocks = jnp.broadcast_to(gains_blocks[:, None], (ndp, nv, 6, part))
    gains_grad = lax.all_to_all(gains_blocks.reshape(seqs, 6, part), ALL, 0, 0, tiled=True)
    gains_grad = gains_grad.sum(0).reshape(3, 2, part)

    first_copy = (v_rank == 0).astype(F32)
    own_squares = (
        jnp.sum(embed_grad * embed_grad)
        + jnp.sum(head_grad * head_grad)
        + first_copy
        * (
            jnp.sum(gains_grad * gains_grad)
            + jnp.sum(entry_grad * entry_grad)
            + jnp.sum(merge_grad * merge_grad)
        )
    )
    total_squares = jnp.sum(all_gather_small(jnp.full((LANES,), own_squares))[:, 0])
    grad_norm = jnp.sqrt(total_squares)
    clip_limit = CLIP_SHARE * DPO_BETA * math.sqrt(COMP * D / (seqs // 2))
    factor = jnp.minimum(1.0, clip_limit / (grad_norm + 1e-06))
    gains_new, gains_first_new, gains_second_new, gains_step = adam_update(
        gains_master, gains_first, gains_second, gains_grad, factor, 0.0
    )
    embed_new, embed_first_new, embed_second_new, embed_step = adam_update(
        embed_master, embed_first, embed_second, embed_grad, factor, WEIGHT_DECAY
    )
    head_new, head_first_new, head_second_new, head_step = adam_update(
        head_master, head_first, head_second, head_grad, factor, WEIGHT_DECAY
    )
    entry_new, entry_first_new, entry_second_new, entry_step = adam_update(
        entry_master, entry_first, entry_second, entry_grad, factor, WEIGHT_DECAY
    )
    merge_new, merge_first_new, merge_second_new, merge_step = adam_update(
        merge_master, merge_first, merge_second, merge_grad, factor, WEIGHT_DECAY
    )
    return (
        loss,
        grad_norm,
        gains_step,
        gains_first_new,
        gains_second_new,
        entry_new,
        entry_first_new,
        entry_second_new,
        entry_new.astype(BF16),
        merge_new,
        merge_first_new,
        merge_second_new,
        merge_new.astype(BF16),
        embed_new,
        embed_first_new,
        embed_second_new,
        embed_new.astype(BF16),
        head_new,
        head_first_new,
        head_second_new,
        head_new.astype(BF16),
    )


def solution(mesh):
    weights = (
        (P(None, None, "dp"),) * 3
        + (P(None, "dp", None),) * 6
        + (P("vocab", "dp"),) * 3
        + (P("dp", "vocab"),) * 3
    )
    placed = weights + (
        P(ALL, None),
        P(ALL),
        P(ALL),
        P(ALL, None),
        P(),
        P(),
    )
    results = (
        (P(), P())
        + (P(None, None, "dp"),) * 3
        + (P(None, "dp", None),) * 8
        + (P("vocab", "dp"),) * 4
        + (P("dp", "vocab"),) * 4
    )
    return jax.shard_map(body, mesh=mesh, in_specs=placed, out_specs=results, check_vma=False)
```

```python
import math
from functools import partial

import jax
import jax.numpy as jnp
import numpy as np
from jax import lax
from jax.experimental import pallas as pl
from jax.experimental.pallas import tpu as pltpu
from jax.sharding import PartitionSpec as P


D = 768
HD = 64
ROT = 16
COMP = 32

DPO_BETA = 0.1
CLIP_SHARE = 0.33
LEARN_RATE = 0.03
WEIGHT_DECAY = 0.1
FIRST_DECAY = 0.9
SECOND_DECAY = 0.95
STEP_NUMBER = 10.0
ADAM_EPSILON = 1e-08
NORM_EPSILON = 1e-05

F32 = jnp.float32
BF16 = jnp.bfloat16
ALL = ("dp", "vocab")
LANES = 128
ACCUMULATORS = 4
EXTRA = 16


def round_up(value, unit):
    return -(-value // unit) * unit


def rounded(values):
    return lax.reduce_precision(values, 8, 7)


def dot(left, right, left_dim, right_dim):
    return lax.dot_general(
        left, right, (((left_dim,), (right_dim,)), ((), ())), preferred_element_type=F32
    )


def gather_kernel(ids_ref, table_ref, out_ref, store, rows):
    total, width = table_ref.shape
    block = out_ref.shape[0]

    @pl.when(pl.program_id(0) == 0)
    def _():
        store[pl.ds(0, total), pl.ds(0, width)] = table_ref[...]
        store[pl.ds(total, 8), :] = jnp.zeros((8, store.shape[1]), F32)

    base = pl.program_id(0) * block

    def step(i, carry):
        first = pl.multiple_of(i * 8, 8)
        for k in range(8):
            rows[pl.ds(first + k, 1), :] = store[pl.ds(ids_ref[base + first + k], 1), :]
        return carry

    lax.fori_loop(0, block // 8, step, 0, unroll=2)
    out_ref[...] = rows[:, :width].astype(out_ref.dtype)


def gather_rows(table, ids, block=1024):
    count = ids.shape[0]
    total, width = table.shape
    return pl.pallas_call(
        gather_kernel,
        out_shape=jax.ShapeDtypeStruct((count, width), BF16),
        grid_spec=pltpu.PrefetchScalarGridSpec(
            num_scalar_prefetch=1,
            grid=(count // block,),
            in_specs=[
                pl.BlockSpec((total, width), lambda i, s: (0, 0), pipeline_mode=pl.Buffered(1))
            ],
            out_specs=pl.BlockSpec((block, width), lambda i, s: (i, 0)),
            scratch_shapes=[
                pltpu.VMEM((total + 8, LANES), F32),
                pltpu.VMEM((block, LANES), F32),
            ],
        ),
        compiler_params=pltpu.CompilerParams(vmem_limit_bytes=50 << 20),
        name="gather_rows",
    )(ids, table)


def scatter_kernel(ids_ref, rows_ref, out_ref, rows, *sums):
    width, total = out_ref.shape
    block = rows_ref.shape[0]
    step_id = pl.program_id(0)

    @pl.when(step_id == 0)
    def _():
        for part in sums:
            part[...] = jnp.zeros_like(part)

    rows[:, pl.ds(0, width)] = rows_ref[...].astype(F32)
    base = step_id * block

    def step(i, carry):
        first = pl.multiple_of(i * 8, 8)
        for k in range(8):
            part = sums[k % len(sums)]
            at = ids_ref[base + first + k]
            part[pl.ds(at, 1), :] = part[pl.ds(at, 1), :] + rows[pl.ds(first + k, 1), :]
        return carry

    lax.fori_loop(0, block // 8, step, 0)

    @pl.when(step_id == pl.num_programs(0) - 1)
    def _():
        for first in range(0, total, LANES):
            size = min(LANES, total - first)
            result = sums[0][pl.ds(first, size), :]
            for part in sums[1:]:
                result = result + part[pl.ds(first, size), :]
            out_ref[:, pl.ds(first, size)] = result.T[:width]


def scatter_rows(rows, ids, total, block):
    count, width = rows.shape
    return pl.pallas_call(
        scatter_kernel,
        out_shape=jax.ShapeDtypeStruct((width, total), F32),
        grid_spec=pltpu.PrefetchScalarGridSpec(
            num_scalar_prefetch=1,
            grid=(count // block,),
            in_specs=[pl.BlockSpec((block, width), lambda i, s: (i, 0))],
            out_specs=pl.BlockSpec(
                (width, total), lambda i, s: (0, 0), pipeline_mode=pl.Buffered(1)
            ),
            scratch_shapes=[pltpu.VMEM((block, LANES), F32)]
            + [pltpu.VMEM((total + 8, LANES), F32) for _ in range(ACCUMULATORS)],
        ),
        compiler_params=pltpu.CompilerParams(vmem_limit_bytes=55 << 20),
        name="scatter_rows",
    )(ids, rows)


def flip(value, bit):
    count = lax.axis_size("vocab")
    return lax.ppermute(value, "vocab", [(i, i ^ bit) for i in range(count)])


def dp_swap(blocks):
    return lax.all_to_all(blocks, "dp", 0, 0, tiled=True)


def dp_gather(value):
    count = lax.axis_size("dp")
    return dp_swap(jnp.broadcast_to(value[None], (count,) + value.shape))


def all_gather_small(value):
    count = lax.axis_size("dp") * lax.axis_size("vocab")
    copies = jnp.broadcast_to(value[None], (count,) + value.shape)
    return lax.all_to_all(copies, ALL, 0, 0, tiled=True)


def window(axis, index, size):
    start = pl.multiple_of(index * size, math.gcd(size, LANES))
    return (pl.ds(start, size), slice(None)) if axis == 0 else (slice(None), pl.ds(start, size))


def split_kernel(me_ref, source, *outs, axis, size, count):
    for k in range(count):
        outs[k][...] = source[window(axis, lax.rem(me_ref[0] + k, count), size)]


def join_kernel(me_ref, *refs, axis, size, count):
    parts, out = refs[:count], refs[count]
    for k in range(count):
        out[window(axis, lax.rem(me_ref[0] + count - k, count), size)] = parts[k][...]


def vmem_call(kernel, outs, scalars, operands, scratch=()):
    def spec(array):
        return pl.BlockSpec(
            array.shape, lambda i, s: (0,) * array.ndim, pipeline_mode=pl.Buffered(1)
        )

    return pl.pallas_call(
        kernel,
        out_shape=outs,
        grid_spec=pltpu.PrefetchScalarGridSpec(
            num_scalar_prefetch=1,
            grid=(1,),
            in_specs=[spec(operand) for operand in operands],
            out_specs=jax.tree.map(spec, outs),
            scratch_shapes=list(scratch),
        ),
        compiler_params=pltpu.CompilerParams(vmem_limit_bytes=50 << 20),
    )(jnp.stack([scalar.astype(jnp.int32) for scalar in scalars]), *operands)


def split_parts(value, axis, size):
    count = lax.axis_size("dp")
    shape = (size, value.shape[1]) if axis == 0 else (value.shape[0], size)
    outs = [jax.ShapeDtypeStruct(shape, value.dtype)] * count
    kernel = partial(split_kernel, axis=axis, size=size, count=count)
    return vmem_call(kernel, outs, [lax.axis_index("dp")], [value])


def join_parts(parts, axis, size):
    count = len(parts)
    rows, cols = parts[0].shape
    shape = (size * count, cols) if axis == 0 else (rows, size * count)
    kernel = partial(join_kernel, axis=axis, size=size, count=count)
    out = jax.ShapeDtypeStruct(shape, parts[0].dtype)
    return vmem_call(kernel, out, [lax.axis_index("dp")], list(parts))


def dp_swap_wide(value, axis):
    count = lax.axis_size("dp")
    size = value.shape[axis] // count
    if count > 8:
        if axis == 0:
            got = dp_swap(value.reshape(count, size, -1))
            return got.transpose(1, 0, 2).reshape(size, -1)
        got = dp_swap(value.reshape(-1, count, size).transpose(1, 0, 2))
        return got.reshape(-1, size)
    parts = split_parts(value, axis, size)
    moved = [parts[0]]
    for shift in range(1, count):
        moved.append(
            lax.ppermute(parts[shift], "dp", [(i, (i + shift) % count) for i in range(count)])
        )
    return join_parts(moved, 1 - axis, value.shape[1 - axis])


def after(value, *others):
    return lax.optimization_barrier((value,) + others)[0]


def vocab_reduce(values):
    values = values[0].astype(F32) + flip(values[1].astype(BF16), 1).astype(F32)
    return values[0] + flip(values[1].astype(BF16), 2).astype(F32)


def vocab_gather(value):
    value = jnp.stack([value, flip(value, 2)])
    return jnp.stack([value, flip(value, 1)])


def normalize(values):
    centre = jnp.mean(values, -1, keepdims=True)
    centred = values - centre
    inverse = lax.rsqrt(jnp.mean(centred * centred, -1, keepdims=True) + NORM_EPSILON)
    return (centred * inverse, inverse)


def norm_back(grad_hat, normed, inverse):
    return inverse * (
        grad_hat
        - jnp.mean(grad_hat, -1, keepdims=True)
        - normed * jnp.mean(grad_hat * normed, -1, keepdims=True)
    )


def rope_tables(length):
    half = ROT // 2
    positions = np.arange(length).astype(np.float32)
    frequency = (10000.0 ** (-np.arange(half).astype(np.float32) * 2.0 / ROT)).astype(np.float32)
    angles = (positions[:, None] * frequency[None, :]).astype(np.float32)
    cosine, sine = np.cos(angles), np.sin(angles)
    keep = np.ones((length, HD), np.float32)
    keep[:, :half] = cosine
    keep[:, half:ROT] = cosine
    above = np.zeros((length, HD), np.float32)
    above[:, :half] = -sine
    below = np.zeros((length, HD), np.float32)
    below[:, half:ROT] = sine
    return jnp.asarray(np.stack([keep, above, below]))


def turned(tile, tables, sign):
    half = ROT // 2
    up = pltpu.roll(tile, LANES - half, 1)
    down = pltpu.roll(tile, half, 1)
    return tile * tables[0] + sign * (up * tables[1] + down * tables[2])


def two_heads(tile):
    low = lax.broadcasted_iota(jnp.int32, tile.shape, 1) < HD
    none = jnp.zeros_like(tile)
    return jnp.concatenate([jnp.where(low, tile, none), jnp.where(low, none, tile)], 0)


def one_tile(pair):
    count = pair.shape[0] // 2
    low = lax.broadcasted_iota(jnp.int32, (count, pair.shape[1]), 1) < HD
    return jnp.where(low, pair[:count], pair[count:])


def tile_of(index):
    return slice(None), pl.ds(index * LANES, LANES)


def absolute_tile(index, core_bit, tiles):
    place = lax.rem(index + core_bit * (tiles // 2), tiles)
    return slice(None), pl.ds(pl.multiple_of(place * LANES, LANES), LANES)


def attention_kernel(
    scalars,
    state_ref,
    gains_ref,
    own_ref,
    other_ref,
    tables_ref,
    mixed_ref,
    state_sel_ref,
    queries_ref,
    keys_ref,
    values_ref,
    weights_ref,
    attn_in_ref,
    attn_sel_ref,
    normed_ref,
    inverse_ref,
    full_rows,
    sel_rows,
    sel_state,
    sel_tables,
):
    row0, core_bit = scalars[0], scalars[1]
    length = state_ref.shape[0]
    half = D // 2
    tiles = D // LANES
    state = state_ref[...].astype(F32)
    normed, inverse = normalize(state)
    normed_ref[...] = normed
    inverse_ref[...] = jnp.broadcast_to(inverse, inverse_ref.shape)
    full_rows[...] = state
    for i in range(COMP):
        sel_state[pl.ds(i, 1), :] = full_rows[pl.ds(row0 + i, 1), :]
        for j in range(3):
            sel_tables[j, pl.ds(i, 1), :] = tables_ref[j, pl.ds(row0 + i, 1), :]
    state_sel_ref[...] = sel_state[...].astype(BF16)
    attn_in = normed * gains_ref[pl.ds(0, 1), :] + gains_ref[pl.ds(1, 1), :]
    full_rows[...] = attn_in
    for i in range(COMP):
        sel_rows[pl.ds(i, 1), :] = full_rows[pl.ds(row0 + i, 1), :]
    attn_in = attn_in.astype(BF16)
    attn_in_ref[...] = attn_in
    attn_sel = sel_rows[...].astype(BF16)
    attn_sel_ref[...] = attn_sel
    tables = [tables_ref[j] for j in range(3)]
    tables_sel = [sel_tables[j] for j in range(3)]
    slot = lax.broadcasted_iota(jnp.int32, (2 * COMP, length), 1)
    row = lax.rem(lax.broadcasted_iota(jnp.int32, (2 * COMP, length), 0), COMP)
    allowed = slot <= row0 + row
    for h, weight_ref in enumerate((own_ref, other_ref)):
        query_half = jnp.dot(attn_sel, weight_ref[:, :half], preferred_element_type=F32)
        kv_half = jnp.dot(attn_in, weight_ref[:, half:], preferred_element_type=F32)
        for t in range(tiles // 2):
            j = h * (tiles // 2) + t
            low, high = t * LANES, (t + 1) * LANES
            query = turned(query_half[:, low:high], tables_sel, 1.0).astype(BF16)
            key = turned(kv_half[:, low:high], tables, 1.0).astype(BF16)
            value = kv_half[:, half + low : half + high].astype(BF16)
            queries_ref[tile_of(j)] = query
            keys_ref[tile_of(j)] = key
            values_ref[tile_of(j)] = value
            scores = dot(two_heads(query), key, 1, 1) * (HD ** (-0.5))
            scores = jnp.where(allowed, scores, -1e30)
            weights = jnp.exp(scores - jnp.max(scores, -1, keepdims=True))
            weights = weights / jnp.sum(weights, -1, keepdims=True)
            weights_ref[pl.ds(j * 2 * COMP, 2 * COMP), :] = weights
            pair = jnp.dot(weights.astype(BF16), value, preferred_element_type=F32)
            mixed_ref[absolute_tile(j, core_bit, tiles)] = one_tile(pair).astype(BF16)


def attention(row0, core_bit, state, gains, own, other, tables):
    length = state.shape[0]
    tiles = D // LANES
    outs = [
        jax.ShapeDtypeStruct((COMP, D), BF16),
        jax.ShapeDtypeStruct((COMP, D), BF16),
        jax.ShapeDtypeStruct((COMP, D), BF16),
        jax.ShapeDtypeStruct((length, D), BF16),
        jax.ShapeDtypeStruct((length, D), BF16),
        jax.ShapeDtypeStruct((tiles * 2 * COMP, length), F32),
        jax.ShapeDtypeStruct((length, D), BF16),
        jax.ShapeDtypeStruct((COMP, D), BF16),
        jax.ShapeDtypeStruct((length, D), F32),
        jax.ShapeDtypeStruct((length, LANES), F32),
    ]
    scratch = [
        pltpu.VMEM((length, D), F32),
        pltpu.VMEM((COMP, D), F32),
        pltpu.VMEM((COMP, D), F32),
        pltpu.VMEM((3, COMP, LANES), F32),
    ]
    return vmem_call(
        attention_kernel, outs, [row0, core_bit], [state, gains, own, other, tables], scratch
    )


def attention_back_kernel(
    scalars,
    grad_mixed_ref,
    grad_mlp_ref,
    grad_next_ref,
    final_pair_ref,
    gains_ref,
    own_ref,
    other_ref,
    tables_ref,
    queries_ref,
    keys_ref,
    values_ref,
    weights_ref,
    attn_in_ref,
    attn_sel_ref,
    normed_ref,
    inverse_ref,
    state_out,
    own_out,
    other_out,
    rows,
    sel_normed,
    sel_tables,
    grad_keys,
    grad_values,
    grad_queries,
):
    row0, core_bit = scalars[0], scalars[1]
    length = normed_ref.shape[0]
    half = D // 2
    tiles = D // LANES
    for i in range(COMP):
        sel_normed[pl.ds(i, 1), :] = normed_ref[pl.ds(row0 + i, 1), :]
        for j in range(3):
            sel_tables[j, pl.ds(i, 1), :] = tables_ref[j, pl.ds(row0 + i, 1), :]
    tables = [tables_ref[j] for j in range(3)]
    tables_sel = [sel_tables[j] for j in range(3)]
    scaling = HD ** (-0.5)
    for j in range(tiles):
        grad_pair = two_heads(grad_mixed_ref[absolute_tile(j, core_bit, tiles)])
        query_pair = two_heads(queries_ref[tile_of(j)])
        key = keys_ref[tile_of(j)]
        value = values_ref[tile_of(j)]
        weights = weights_ref[pl.ds(j * 2 * COMP, 2 * COMP), :]
        grad_values[tile_of(j)] = dot(weights.astype(BF16), grad_pair, 0, 0).astype(BF16)
        grad_weights = dot(grad_pair, value, 1, 1)
        grad_scores = (
            weights * (grad_weights - jnp.sum(weights * grad_weights, -1, keepdims=True))
        ).astype(BF16)
        grad_query = one_tile(jnp.dot(grad_scores, key, preferred_element_type=F32)) * scaling
        grad_key = dot(grad_scores, query_pair, 0, 0) * scaling
        grad_queries[tile_of(j)] = turned(grad_query, tables_sel, -1.0).astype(BF16)
        grad_keys[tile_of(j)] = turned(grad_key, tables, -1.0).astype(BF16)
    attn_in_t = attn_in_ref[...].T
    attn_sel_t = attn_sel_ref[...].T
    grad_in = jnp.zeros((length, D), F32)
    grad_sel = jnp.zeros((COMP, D), F32)
    for h, (weight_ref, out) in enumerate(((own_ref, own_out), (other_ref, other_out))):
        columns = slice(h * half, (h + 1) * half)
        key_half = grad_keys[:, columns]
        value_half = grad_values[:, columns]
        query_half = grad_queries[:, columns]
        grad_in += dot(key_half, weight_ref[:, half : 2 * half], 1, 1)
        grad_in += dot(value_half, weight_ref[:, 2 * half :], 1, 1)
        grad_sel += dot(query_half, weight_ref[:, :half], 1, 1)
        out[:, :half] = jnp.dot(
            attn_sel_t, query_half, preferred_element_type=F32
        ).astype(out.dtype)
        out[:, half : 2 * half] = jnp.dot(
            attn_in_t, key_half, preferred_element_type=F32
        ).astype(out.dtype)
        out[:, 2 * half :] = jnp.dot(
            attn_in_t, value_half, preferred_element_type=F32
        ).astype(out.dtype)

    def add_rows(values):
        for i in range(COMP):
            at = pl.ds(row0 + i, 1)
            rows[at, :] = rows[at, :] + values[i : i + 1, :]

    normed = normed_ref[...]
    grad_mlp = grad_mlp_ref[...]
    rows[...] = grad_in
    add_rows(grad_sel)
    grad_in = rows[...]
    sums = [
        jnp.sum(grad_in * normed, 0, keepdims=True),
        jnp.sum(grad_in, 0, keepdims=True),
        jnp.sum(grad_mlp * sel_normed[...], 0, keepdims=True),
        jnp.sum(grad_mlp, 0, keepdims=True),
        final_pair_ref[...],
        jnp.zeros((state_out.shape[0] - length - 6, D), F32),
    ]
    state_out[pl.ds(length, state_out.shape[0] - length), :] = jnp.concatenate(sums, 0).astype(
        BF16
    )
    rows[...] = grad_in * gains_ref[pl.ds(0, 1), :]
    add_rows(grad_mlp * gains_ref[pl.ds(2, 1), :])
    rows[...] = norm_back(rows[...], normed, inverse_ref[:, :1])
    add_rows(grad_next_ref[...])
    state_out[pl.ds(0, length), :] = rows[...].astype(BF16)


def attention_back(row0, core_bit, grads, gains, own, other, tables, kept):
    length = kept[1].shape[0]
    outs = [
        jax.ShapeDtypeStruct((length + EXTRA, D), BF16),
        jax.ShapeDtypeStruct(own.shape, F32),
        jax.ShapeDtypeStruct(own.shape, BF16),
    ]
    scratch = [
        pltpu.VMEM((length, D), F32),
        pltpu.VMEM((COMP, D), F32),
        pltpu.VMEM((3, COMP, LANES), F32),
        pltpu.VMEM((length, D), BF16),
        pltpu.VMEM((length, D), BF16),
        pltpu.VMEM((COMP, D), BF16),
    ]
    return vmem_call(
        attention_back_kernel,
        outs,
        [row0, core_bit],
        [*grads, gains, own, other, tables, *kept],
        scratch,
    )


def exact_gelu(values):
    return jax.nn.gelu(values, approximate=False)


def adam_update(master, first_moment, second_moment, gradient, factor, decay_rate):
    scaled = gradient * factor
    new_first = FIRST_DECAY * first_moment + (1.0 - FIRST_DECAY) * scaled
    new_second = SECOND_DECAY * second_moment + (1.0 - SECOND_DECAY) * scaled * scaled
    first_hat = new_first / (1.0 - FIRST_DECAY**STEP_NUMBER)
    second_hat = new_second / (1.0 - SECOND_DECAY**STEP_NUMBER)
    change = -LEARN_RATE * (first_hat / (jnp.sqrt(second_hat) + ADAM_EPSILON) + decay_rate * master)
    new_master = master + change
    return (new_master, new_first, new_second, change)


def step(
    gains_master,
    gains_first,
    gains_second,
    entry_master,
    entry_first,
    entry_second,
    merge_master,
    merge_first,
    merge_second,
    embed_master,
    embed_first,
    embed_second,
    head_master,
    head_first,
    head_second,
    tokens,
    seq_lengths,
    answer_len,
    ref_logp,
    pairing,
    deal,
):
    ndp = lax.axis_size("dp")
    nv = lax.axis_size("vocab")
    seqs = ndp * nv
    d_rank = lax.axis_index("dp")
    v_rank = lax.axis_index("vocab")
    core_bit = v_rank % 2
    cross_bit = v_rank // 2
    length = tokens.shape[1]
    part = D // ndp
    quarter = embed_master.shape[0]
    merge_rows = merge_master.shape[1]
    merge_cols = round_up(merge_rows, 2 * LANES)
    head_cols = round_up(-(-head_master.shape[1] // ndp), LANES)
    entry = entry_master[0].astype(BF16)
    merge = merge_master[0].astype(BF16)

    half = D // 2
    own_heads = jnp.concatenate(
        [
            lax.dynamic_slice_in_dim(entry, i * D + core_bit * half, half, 1)
            for i in range(3)
        ],
        1,
    )
    qkv_own = lax.all_gather(own_heads, "dp", axis=0, tiled=True)

    def both_cores(own_value, other_value):
        first = jnp.where(core_bit == 0, own_value, other_value)
        second = jnp.where(core_bit == 0, other_value, own_value)
        return jnp.concatenate([first, second], 1)

    pieces = [
        tokens.reshape(-1).astype(F32),
        rounded(gains_master).reshape(-1),
        ref_logp.reshape(-1),
        seq_lengths.astype(F32),
        answer_len.astype(F32),
    ]
    packed = jnp.concatenate(pieces)
    filled = packed.shape[0]
    packed = jnp.pad(packed, (0, round_up(filled, 8 * LANES) - filled)).reshape(-1, LANES)
    shared = all_gather_small(packed).reshape(seqs, -1)
    up_blocks = after(entry, shared)[:, 2 * D :].reshape(part, ndp, merge_rows)
    up_weight = dp_swap(up_blocks.transpose(1, 0, 2)).reshape(D, merge_rows)
    at = length
    load_tokens = shared[:, :at].astype(jnp.int32)
    gains_count = 6 * part
    gains_full = (
        shared.reshape(ndp, nv, -1)[:, 0, at : at + gains_count]
        .reshape(ndp, 3, 2, part)
        .transpose(1, 2, 0, 3)
        .reshape(3, 2, D)
    )
    at += gains_count
    ref_all = shared[:, at : at + COMP]
    at += COMP
    load_lengths = shared[:, at].astype(jnp.int32)
    load_live = shared[:, at + 1].astype(jnp.int32)

    offsets = jnp.array([0, 2, 1, 3])
    batch = jnp.arange(seqs)
    seq_rel = (jnp.arange(ndp)[None, :] * nv + (v_rank ^ offsets)[:, None]).reshape(-1)
    rel_of = offsets[v_rank ^ (batch % nv)] * ndp + batch // nv
    batch_start = jnp.take(load_lengths, deal, axis=0) - COMP
    batch_live = jnp.take(load_live, deal, axis=0)
    deal_rel = jnp.take(deal, seq_rel, axis=0)
    tokens_rel = jnp.take(load_tokens, deal_rel, axis=0)
    start_rel = jnp.take(load_lengths, deal_rel, axis=0) - COMP
    own = d_rank * nv + v_rank
    row0 = batch_start[own] - 1

    local = tokens_rel.reshape(-1) - v_rank * quarter
    ids = jnp.where((local >= 0) & (local < quarter), local, quarter)
    found = gather_rows(embed_master, ids).reshape(2, nv // 2, ndp, length, part)
    found = after(vocab_reduce(found).astype(BF16), up_weight)
    state = dp_swap(found).transpose(1, 0, 2).reshape(length, D)
    head_padded = jnp.pad(
        head_master.astype(BF16), ((0, 0), (0, head_cols * ndp - head_master.shape[1]))
    )
    head_weight = dp_swap_wide(after(head_padded, state), 1)

    qkv_own = after(qkv_own, state)
    qkv_other = flip(qkv_own, 1)

    tables = jnp.tile(rope_tables(length), (1, 1, LANES // HD))
    gains_rows = jnp.pad(gains_full.reshape(6, D), ((0, 2), (0, 0)))
    mixed, state_sel, *kept = attention(
        row0, core_bit, state, gains_rows, qkv_own, qkv_other, tables
    )

    mixed_blocks = jnp.pad(mixed, ((0, 0), (0, ndp * merge_rows - D))).reshape(
        COMP, ndp, merge_rows
    )
    sent = jnp.concatenate(
        [
            jnp.broadcast_to(state_sel[None], (ndp, COMP, D)),
            mixed_blocks.transpose(1, 0, 2),
        ],
        2,
    )
    got = dp_swap(sent).reshape(ndp * COMP, D + merge_rows)
    group_normed, _ = normalize(got[:, :D].astype(F32))
    mlp_in = (group_normed * gains_full[1, 0] + gains_full[1, 1]).astype(BF16)
    up_proj = jnp.dot(mlp_in, up_weight, preferred_element_type=F32)
    activated, gelu_pull = jax.vjp(exact_gelu, up_proj)
    is_mlp = (d_rank * merge_rows + jnp.arange(merge_rows) >= D)[None, :]
    joined = jnp.where(is_mlp, activated.astype(BF16), got[:, D:])
    branch = jnp.dot(joined, merge, preferred_element_type=F32)
    branch = dp_swap(branch.astype(BF16).reshape(ndp, COMP, D)).astype(F32).sum(0)

    final_hat, final_inverse = normalize(state_sel.astype(F32) + branch)
    final_gain = gains_full[2, 0]
    comp_rows = (final_hat * final_gain + gains_full[2, 1]).astype(BF16)
    rows = vocab_gather(dp_gather(comp_rows)).reshape(seqs * COMP, D)

    logits = jnp.dot(rows, head_weight, preferred_element_type=F32)
    slots = jnp.arange(length)[None, None, :] == (
        start_rel[:, None, None] + jnp.arange(COMP)[None, :, None]
    )
    targets = jnp.sum(jnp.where(slots, tokens_rel[:, None, :], 0), -1).reshape(-1)
    column = jnp.arange(head_cols)[None, :]
    valid = d_rank * head_cols + column < quarter
    is_target = (
        column + (v_rank * quarter + d_rank * head_cols) == targets[:, None]
    ) & valid
    top_local = jnp.max(jnp.where(valid, logits, -1e30), -1)
    total_local = jnp.sum(jnp.where(valid, jnp.exp(logits - top_local[:, None]), 0.0), -1)
    picked_local = jnp.sum(jnp.where(is_target, logits, 0.0), -1)
    stats = jnp.stack([top_local, total_local, picked_local]).reshape(3, seqs, COMP)
    stats = jnp.take(stats, rel_of, axis=1)
    stats = all_gather_small(stats.reshape(-1, LANES)).reshape(seqs, 3, seqs, COMP)
    top_all = jnp.max(stats[:, 0], 0)
    total_all = jnp.sum(stats[:, 1] * jnp.exp(stats[:, 0] - top_all[None]), 0)
    log_total = top_all + jnp.log(total_all)
    logprob = jnp.sum(stats[:, 2], 0) - log_total
    live = (jnp.arange(COMP)[None, :] < batch_live[:, None]).astype(F32)
    score = jnp.sum(live * (logprob - ref_all), 1)
    chosen = pairing[0::2]
    rejected = pairing[1::2]
    margin = DPO_BETA * (score[chosen] - score[rejected])
    loss = jnp.mean(-jax.nn.log_sigmoid(margin))
    pull = -DPO_BETA * jax.nn.sigmoid(-margin) / margin.shape[0]
    signs = (chosen[None, :] == batch[:, None]).astype(F32) - (
        rejected[None, :] == batch[:, None]
    ).astype(F32)
    coef = jnp.sum(pull[None, :] * signs, 1)
    row_coef = jnp.take(coef[:, None] * live, seq_rel, axis=0).reshape(-1, 1)
    row_total = jnp.take(log_total, seq_rel, axis=0).reshape(-1, 1)
    grad_logits = row_coef * (is_target.astype(F32) - jnp.exp(logits - row_total))
    grad_logits = jnp.where(valid, grad_logits, 0.0).astype(BF16)

    grad_head = dot(rows, grad_logits, 0, 0).astype(BF16)
    head_grad = dp_swap_wide(grad_head, 0)[:, :quarter].astype(F32)
    grad_rows = dot(grad_logits, head_weight, 1, 1).reshape(2, nv // 2, ndp, COMP, D)
    grad_rows = vocab_reduce(grad_rows).astype(BF16)
    grad_final = dp_swap(grad_rows).astype(F32).sum(0)
    final_pair = jnp.stack([jnp.sum(grad_final * final_hat, 0), jnp.sum(grad_final, 0)])
    grad_next = norm_back(grad_final * final_gain, final_hat, final_inverse)

    grad_branch = dp_gather(grad_next.astype(BF16)).reshape(ndp * COMP, D)
    grad_merge = dot(joined, grad_branch, 0, 0)
    grad_joined = dot(grad_branch, merge, 1, 1)
    grad_up = jnp.where(is_mlp, gelu_pull(grad_joined)[0], 0.0).astype(BF16)
    grad_up_weight = dot(mlp_in, grad_up, 0, 0)
    grad_mlp = dot(grad_up, up_weight, 1, 1)
    sent = jnp.concatenate([grad_mlp.astype(BF16), grad_joined.astype(BF16)], 1)
    got = dp_swap(sent.reshape(ndp, COMP, D + merge_rows))
    grad_mlp_in = got[:, :, :D].astype(F32).sum(0)
    grad_mixed = got[:, :, D:].transpose(1, 0, 2).reshape(COMP, ndp * merge_rows)[:, :D]

    state_out, qkv_own_grad, qkv_other_grad = attention_back(
        row0,
        core_bit,
        [grad_mixed, grad_mlp_in, grad_next, final_pair],
        gains_rows,
        qkv_own,
        qkv_other,
        tables,
        kept,
    )

    height = length + EXTRA
    state_blocks = state_out.reshape(height, ndp, part).transpose(1, 0, 2)
    state_rows = dp_swap(state_blocks)
    state_rows = vocab_gather(state_rows)
    gains_grad = state_rows[..., length : length + 6, :].astype(F32).sum((0, 1, 2))
    gains_grad = gains_grad.reshape(3, 2, part)
    scatter_ids = jnp.pad(
        ids.reshape(seqs, length), ((0, 0), (0, EXTRA)), constant_values=quarter
    ).reshape(-1)
    embed_grad = scatter_rows(state_rows.reshape(-1, part), scatter_ids, quarter, 4 * height)

    def core_half(value, index):
        size = value.shape[-1] // 2
        return lax.dynamic_slice_in_dim(value, index * size, size, value.ndim - 1)

    def core_reduce(value):
        other = core_half(value, 1 - core_bit).astype(BF16)
        return core_half(value, core_bit) + flip(other, 1).astype(F32)

    def cross_reduce(value):
        size = value.shape[-2] // 2
        at_rows = value.ndim - 2
        other = lax.dynamic_slice_in_dim(value, (1 - cross_bit) * size, size, at_rows)
        kept = lax.dynamic_slice_in_dim(value, cross_bit * size, size, at_rows)
        return kept + flip(other.astype(BF16), 2).astype(F32)

    merge_part = cross_reduce(core_reduce(grad_merge)).astype(BF16)
    up_part = core_reduce(jnp.pad(grad_up_weight, ((0, 0), (0, merge_cols - merge_rows))))
    up_part = cross_reduce(up_part.reshape(ndp, part, merge_cols // 2)).astype(BF16)
    qkv_width = 3 * half
    qkv_part = qkv_own_grad + flip(qkv_other_grad, 1).astype(F32)
    qkv_part = cross_reduce(qkv_part.reshape(ndp, part, qkv_width)).astype(BF16)
    got = dp_swap(jnp.concatenate([qkv_part, up_part], 2))
    qkv_part = got[:, :, :qkv_width].astype(F32).sum(0).astype(BF16)
    up_part = got[:, :, qkv_width:].transpose(1, 0, 2).reshape(part // 2, -1)
    quarter_grad = jnp.concatenate([qkv_part, up_part], 1)
    squares = (
        jnp.sum(jnp.square(embed_grad))
        + jnp.sum(jnp.square(head_grad))
        + jnp.sum(jnp.square(merge_part.astype(F32)))
        + jnp.sum(jnp.square(quarter_grad.astype(F32)))
        + (v_rank == 0).astype(F32) * jnp.sum(jnp.square(gains_grad))
    )

    def rows_of_both(value):
        other = flip(value, 2)
        first = jnp.where(cross_bit == 0, value, other)
        second = jnp.where(cross_bit == 0, other, value)
        return jnp.concatenate([first, second], 0)

    merge_half = rows_of_both(merge_part)
    merge_grad = both_cores(merge_half, flip(merge_half, 1)).astype(F32)[None]
    quarter_half = rows_of_both(quarter_grad)
    other = flip(quarter_half, 1)
    first = jnp.where(core_bit == 0, quarter_half, other)
    second = jnp.where(core_bit == 0, other, quarter_half)
    qkv_grad = jnp.concatenate(
        [side[:, i * half : (i + 1) * half] for i in range(3) for side in (first, second)], 1
    )
    up_grad = jnp.concatenate(
        [side[:, qkv_width:].reshape(part, ndp, -1) for side in (first, second)], 2
    )
    up_grad = up_grad[:, :, :merge_rows].reshape(part, -1)[:, D:]
    entry_grad = jnp.concatenate([qkv_grad, up_grad], 1).astype(F32)[None]

    total_squares = jnp.sum(all_gather_small(jnp.full((LANES,), squares))[:, 0])
    grad_norm = jnp.sqrt(total_squares)
    clip_limit = CLIP_SHARE * DPO_BETA * math.sqrt(COMP * D / (seqs // 2))
    factor = jnp.minimum(1.0, clip_limit / (grad_norm + 1e-06))
    _, gains_first_new, gains_second_new, gains_step = adam_update(
        gains_master, gains_first, gains_second, gains_grad, factor, 0.0
    )
    embed_new, embed_first_new, embed_second_new, _ = adam_update(
        embed_master.T, embed_first.T, embed_second.T, embed_grad, factor, WEIGHT_DECAY
    )
    head_new, head_first_new, head_second_new, _ = adam_update(
        head_master, head_first, head_second, head_grad, factor, WEIGHT_DECAY
    )
    entry_new, entry_first_new, entry_second_new, _ = adam_update(
        entry_master, entry_first, entry_second, entry_grad, factor, WEIGHT_DECAY
    )
    merge_new, merge_first_new, merge_second_new, _ = adam_update(
        merge_master, merge_first, merge_second, merge_grad, factor, WEIGHT_DECAY
    )
    return (
        loss,
        grad_norm,
        gains_step,
        gains_first_new,
        gains_second_new,
        entry_new,
        entry_first_new,
        entry_second_new,
        entry_new.astype(BF16),
        merge_new,
        merge_first_new,
        merge_second_new,
        merge_new.astype(BF16),
        embed_new.T,
        embed_first_new.T,
        embed_second_new.T,
        embed_new.astype(BF16).T,
        head_new,
        head_first_new,
        head_second_new,
        head_new.astype(BF16),
    )


def solution(mesh):
    weights = (
        (P(None, None, "dp"),) * 3
        + (P(None, "dp", None),) * 6
        + (P("vocab", "dp"),) * 3
        + (P("dp", "vocab"),) * 3
    )
    placed = weights + (
        P(ALL, None),
        P(ALL),
        P(ALL),
        P(ALL, None),
        P(),
        P(),
    )
    results = (
        (P(), P())
        + (P(None, None, "dp"),) * 3
        + (P(None, "dp", None),) * 8
        + (P("vocab", "dp"),) * 4
        + (P("dp", "vocab"),) * 4
    )
    return jax.shard_map(step, mesh=mesh, in_specs=placed, out_specs=results, check_vma=False)
```
